768 devices in a mesh: grp: 96 (over y_lo, z, x), fsdp: 8 (over y_hi, core).
Axes of the slice: x: 4, y: 8 (y_hi: 4, y_lo: 2; y = y_hi * 2 + y_lo), z: 12, core: 2. Of those that a mesh axis runs over, the one named last changes fastest.
Arguments:
- text: bfloat16 [98304, 8192], P(('grp', 'fsdp'))
- vision: bfloat16 [12288, 8192], P(('grp', 'fsdp'))
- vision_token: int32 [12288], P(('grp', 'fsdp')), may hold values from 0 to 98303, as said below
- gain: bfloat16 [8192], P('fsdp'), may hold values from 0.099609375 to 1.8984375
- cotangent: bfloat16 [98304, 8192], P(('grp', 'fsdp')), may hold values from -6 to 6
Outputs:
- vision_grad: bfloat16 [12288, 8192], P(('grp', 'fsdp'))
- gain_grad: float32 [8192], P('fsdp')
The draws below stay inside these ranges and needn't reach their ends.
Inputs may be any that keep to these rules, and one draw needn't show every extreme that they name: `vision_token`: device d of the flattened grp+fsdp order holds vision rows d * 16 to (d + 1) * 16 - 1 and token rows d * 128 to (d + 1) * 128 - 1. The rows held in group g go to tokens of group (g + 24) mod 96; a device sends at most 4 rows to any one device, and in every group some device receives exactly 4 rows from every device of its source group. No token receives two rows.
All inputs are finite; a program needn't handle non-finite values.
Results may differ from the reference program's by a relative error of at most 0.001.
Values may be sent and summed in bfloat16 or wider, within the bound.
No kernel may reach another device: no remote copies, remote signals or barrier semaphores. Data moves between devices by JAX's collectives and lax.ppermute only.
A program may use at most 32 MiB of HBM per device.

```python
import jax
import jax.numpy as jnp
from jax import lax

D = 8192
TOK_DEV = 128
VIS_DEV = 16
CAP = 4
TOKENS = 98304
N_GRP = 96
N_FSDP = 8


def column_scales(key):
    return jnp.exp(jax.random.uniform(jax.random.fold_in(key, 11), (D,), jnp.float32, -1.15, 1.15))


def scaled_rows(key, count, salt):
    keyed = jax.random.fold_in(key, salt)
    first, second = jax.random.split(keyed, 2)
    base = jax.random.normal(first, (count, D), jnp.float32)
    row_scale = jnp.exp(jax.random.uniform(second, (count, 1), jnp.float32, -1.15, 1.15))
    return base * row_scale * column_scales(key)[None, :]


def draw_text(key, part):
    return scaled_rows(key, TOK_DEV * N_GRP * N_FSDP, 3).astype(jnp.bfloat16)


def draw_vision(key, part):
    return scaled_rows(key, VIS_DEV * N_GRP * N_FSDP, 5).astype(jnp.bfloat16)


def draw_vision_token(key, part):
    keyed = jax.random.fold_in(key, 29)
    key_hot, key_score, key_order, key_place = jax.random.split(keyed, 4)
    sources = N_GRP * N_FSDP
    slots = N_FSDP * CAP
    hot = jax.random.randint(key_hot, (N_GRP,), 0, N_FSDP)
    source_ids = jnp.arange(sources)
    source_group = source_ids // N_FSDP
    source_index = source_ids % N_FSDP
    target_group = (source_group + N_GRP // 4) % N_GRP
    hot_source = hot[target_group]
    slot_ids = jnp.arange(slots)
    score = jax.random.randint(key_score, (sources, slots), 0, 2 ** 20) * slots + slot_ids[None, :]
    score = jnp.where((slot_ids // CAP)[None, :] == hot_source[:, None], score - 2 ** 30, score)
    chosen = jnp.argsort(score, axis=1)[:, :VIS_DEV]
    order_score = jax.random.randint(key_order, (sources, VIS_DEV), 0, 2 ** 20) * VIS_DEV + jnp.arange(VIS_DEV)[None, :]
    chosen = jnp.take_along_axis(chosen, jnp.argsort(order_score, axis=1), axis=1)
    target = chosen // CAP
    within = chosen % CAP
    place_score = jax.random.randint(key_place, (sources, TOK_DEV), 0, 2 ** 20) * TOK_DEV + jnp.arange(TOK_DEV)[None, :]
    places = jnp.argsort(place_score, axis=1)
    target_device = target_group[:, None] * N_FSDP + target
    rank = source_index[:, None] * CAP + within
    position = places[target_device, rank]
    return (target_device * TOK_DEV + position).reshape(-1).astype(jnp.int32)


def levels(own_key, extent, pieces, smallest, high):
    level = 1.0
    for dim, parts in pieces:
        draws = jax.random.uniform(jax.random.fold_in(jax.random.fold_in(own_key, 6), dim), (parts,), jnp.float32, smallest / len(pieces), high / len(pieces))
        level = level * jnp.repeat(jnp.exp(draws), extent[dim] // parts).reshape((-1,) + (1,) * (len(extent) - 1 - dim))
    return level


def scatter_about(stream_key, extent, spread, limit, pieces=(), held_as=jnp.bfloat16):
    result = jax.random.normal(stream_key, extent, jnp.float32) * spread
    if len(pieces) > 0:
        result = levels(stream_key, extent, pieces, -0.22, 0.18) * result
    return jnp.clip(result, min=-limit, max=limit).astype(held_as)


def setup_inputs(seed: int = 0) -> dict:
    splits = jax.random.split(jax.random.key(seed), 6)
    text = draw_text(jax.random.fold_in(splits[5], 71), 0)
    vision = draw_vision(jax.random.fold_in(splits[5], 71), 0)
    vision_token = draw_vision_token(jax.random.fold_in(splits[5], 71), 0)
    gain = jnp.clip(1.0 + 0.18 * jax.random.normal(splits[3], (D,), jnp.float32), 0.099609375, 1.8984375).astype(jnp.bfloat16)
    cotangent = scatter_about(splits[4], (TOKENS, D), 1.0, 6.0, ((0, 768),))
    return {"text": text, "vision": vision, "vision_token": vision_token, "gain": gain, "cotangent": cotangent}


def reference(text, vision, vision_token, gain, cotangent):
    assembled = text.at[vision_token].set(vision)
    scale_row = gain.astype(jnp.float32)
    blocks = assembled.reshape(-1, TOK_DEV, D)
    cot_blocks = cotangent.reshape(-1, TOK_DEV, D)

    def advance(total, pair):
        rows, grads = pair
        values = rows.astype(jnp.float32)
        upper = grads.astype(jnp.float32)
        inv = lax.rsqrt(lax.optimization_barrier(jnp.mean(values * values, axis=-1, keepdims=True)) + 1e-06)
        scaled = upper * scale_row
        inner = lax.optimization_barrier(jnp.mean(values * scaled, axis=-1, keepdims=True))
        token_grad = inv * scaled - values * inv * inv * inv * inner
        total = total + lax.optimization_barrier(jnp.sum(upper * values * inv, axis=0))
        return (total, token_grad.astype(jnp.bfloat16))
    total, token_grad = lax.scan(advance, jnp.zeros((D,), jnp.float32), (blocks, cot_blocks))
    token_grad = token_grad.reshape(-1, D)
    return (token_grad[vision_token], total)
```

```python
import jax
import jax.numpy as jnp
from jax import lax
from jax.sharding import Mesh, PartitionSpec as P

AXES = ("ylo", "zhi", "zlo", "x", "yhi", "core")
QUARTER = ("ylo", "zhi")
GRP = ("ylo", "zhi", "zlo", "x")
FSDP = ("yhi", "core")
PLANE = ("yhi", "core", "ylo", "x")
SIZES = (2, 2, 6, 4, 4, 2)
N_QUARTER = 4
N_FSDP = 8
CAP = 4


def exchange(value, axes):
    return lax.all_to_all(value, axes, split_axis=0, concat_axis=0, tiled=True)


def turned(value, steps):
    pairs = [(source, (source + steps) % N_QUARTER) for source in range(N_QUARTER)]
    return lax.ppermute(value, QUARTER, pairs)


def select_rows(onehot, rows):
    picked = lax.dot_general(
        onehot, rows, (((1,), (0,)), ((), ())), preferred_element_type=jnp.float32
    )
    return picked.astype(rows.dtype)


def shards(text, vision, vision_token, gain, cotangent):
    tok_dev, width = text.shape
    vis_dev = vision.shape[0]
    quarter = lax.axis_index(QUARTER)
    me = lax.axis_index(FSDP)

    tokens = exchange(
        jnp.broadcast_to(vision_token[None, :], (N_QUARTER * N_FSDP, vis_dev)), QUARTER + FSDP
    ).reshape(N_QUARTER, N_FSDP, vis_dev)
    from_quarter = (quarter + N_QUARTER - 1) % N_QUARTER
    tokens = jnp.sum(
        jnp.where(jnp.arange(N_QUARTER)[:, None, None] == from_quarter, tokens, 0), axis=0
    )
    rows = turned(vision, 1)
    full_gain = exchange(jnp.broadcast_to(gain[None, :], (N_FSDP, gain.shape[0])), FSDP)
    full_gain = full_gain.reshape(1, width).astype(jnp.float32)

    target = tokens // tok_dev % N_FSDP
    local = tokens % tok_dev
    same = target[:, :, None] == target[:, None, :]
    before = jnp.arange(vis_dev)[None, :] < jnp.arange(vis_dev)[:, None]
    rank = jnp.sum((same & before[None]).astype(jnp.int32), axis=2)

    sends = (target == me)[:, None, :] & (rank[:, None, :] == jnp.arange(CAP)[None, :, None])
    place = jnp.sum(jnp.where(sends, local[:, None, :] + 1, 0), axis=2).reshape(N_FSDP * CAP, 1) - 1
    pick = place == jnp.arange(tok_dev)[None, :]
    sent = select_rows(pick.astype(jnp.bfloat16), cotangent).reshape(N_FSDP, CAP, width)
    arrived = exchange(sent, FSDP).reshape(N_FSDP * CAP, width)

    values = text.astype(jnp.float32)
    upper = cotangent.astype(jnp.float32)
    inv = lax.rsqrt(jnp.mean(values * values, axis=-1, keepdims=True) + 1e-06)
    kept = jnp.where(jnp.any(pick, axis=0)[:, None], 0.0, inv)
    terms = jnp.sum(upper * values * kept, axis=0)

    mine = jnp.arange(N_FSDP)[:, None] == me
    slot = jnp.sum(jnp.where(mine, target * CAP + rank, 0), axis=0)[:, None]
    order = slot == jnp.arange(N_FSDP * CAP)[None, :]
    upper_v = select_rows(order.astype(jnp.bfloat16), arrived).astype(jnp.float32)
    values_v = rows.astype(jnp.float32)
    inv_v = lax.rsqrt(jnp.mean(values_v * values_v, axis=-1, keepdims=True) + 1e-06)
    scaled = upper_v * full_gain
    inner = jnp.mean(values_v * scaled, axis=-1, keepdims=True)
    grad = inv_v * scaled - values_v * inv_v * inv_v * inv_v * inner
    vision_grad = turned(grad.astype(jnp.bfloat16), -1)
    terms = terms + jnp.sum(upper_v * values_v * inv_v, axis=0)

    lanes = width // 64
    part = jnp.sum(exchange(terms.reshape(64, lanes), PLANE), axis=0)
    parts = exchange(jnp.broadcast_to(part[None, :], (96, lanes)), GRP)
    gain_grad = jnp.sum(parts.reshape(2, 12, 4, lanes), axis=1).reshape(width // N_FSDP)
    return (vision_grad, gain_grad)


def solution(mesh):
    fine = Mesh(mesh.devices.reshape(SIZES), AXES)
    return jax.shard_map(
        shards,
        mesh=fine,
        in_specs=(P(AXES, None), P(AXES, None), P(AXES), P(FSDP), P(AXES, None)),
        out_specs=(P(AXES, None), P(FSDP)),
        check_vma=False,
    )
```

```python
import jax
import jax.numpy as jnp
from jax import lax
from jax.experimental import pallas as pl
from jax.experimental.pallas import tpu as pltpu
from jax.sharding import Mesh, PartitionSpec as P

AXES = ("ylo", "zhi", "zlo", "x", "yhi", "core")
QUARTER = ("ylo", "zhi")
GRP = ("ylo", "zhi", "zlo", "x")
FSDP = ("yhi", "core")
PLANE = ("yhi", "core", "ylo", "x")
SIZES = (2, 2, 6, 4, 4, 2)
DEVICES = 768
N_QUARTER = 4
N_FSDP = 8
CAP = 4
TOK = 128
VIS = 16
WIDTH = 8192
HALF = WIDTH // 2
LANES = 128
SLOTS = N_FSDP * 2 * CAP
BLOCKS = WIDTH // LANES
F32 = jnp.float32
BF16 = jnp.bfloat16
VMEM = pl.BlockSpec(memory_space=pltpu.VMEM)
SMEM = pl.BlockSpec(memory_space=pltpu.SMEM)


def iota(shape, dim):
    return lax.broadcasted_iota(jnp.int32, shape, dim)


def dot(a, b):
    return jnp.dot(a, b, preferred_element_type=F32)


def pack_kernel(dev_ref, tok_ref, gain_ref, cot_ref, sent_ref, order_ref, taken_ref):
    dev = dev_ref[0]
    source = lax.rem(dev // (DEVICES // N_QUARTER) + N_QUARTER - 1, N_QUARTER) * N_FSDP
    tokens = tok_ref[pl.ds(pl.multiple_of(source, N_FSDP), N_FSDP), :]
    position = dev * TOK + iota((N_FSDP, TOK), 1)
    count = jnp.zeros((N_FSDP, TOK), jnp.int32)
    chosen = [jnp.zeros((N_FSDP, TOK), F32)] * CAP
    for i in range(VIS):
        token = jnp.broadcast_to(tokens[:, i : i + 1], (N_FSDP, TOK))
        hit = token == position
        for r in range(CAP):
            chosen[r] = jnp.where(hit & (count == r), 1.0, chosen[r])
        count = count + jnp.where((token >> 7) == dev, 1, 0)
    chosen = jnp.concatenate(chosen, axis=0)
    taken_ref[...] = jnp.broadcast_to(jnp.sum(chosen, axis=0, keepdims=True), taken_ref.shape)
    chosen = chosen.astype(BF16)
    row, col = iota((SLOTS, N_FSDP * CAP), 0), iota((SLOTS, N_FSDP * CAP), 1)
    halves = []
    for half in range(2):
        at = ((col & 7) == (row >> 3)) & ((col >> 3) + CAP * half == (row & 7))
        halves.append(dot(jnp.where(at, 1.0, 0.0).astype(BF16), chosen).astype(BF16))
    lhs = jnp.concatenate(halves, axis=1)
    step = 512
    for k in range(0, HALF, step):
        rhs = jnp.concatenate([cot_ref[:, k : k + step], cot_ref[:, HALF + k : HALF + k + step]], axis=0)
        sent_ref[:, k : k + step] = dot(lhs, rhs).astype(BF16)
    gain = gain_ref[...].astype(F32)
    sent_ref[:, HALF:] = jnp.concatenate([gain] * N_FSDP, axis=0).astype(BF16)
    own = jnp.broadcast_to(tok_ref[pl.ds(source + lax.rem(dev, N_FSDP), 1), :], (VIS, VIS))
    i, j = iota((VIS, VIS), 0), iota((VIS, VIS), 1)
    target = ((own >> 7) & (N_FSDP - 1)).astype(F32)
    mine = jnp.sum(jnp.where(i == j, target, 0.0), axis=1, keepdims=True)
    rank = jnp.sum(jnp.where((target == mine) & (j < i), 1.0, 0.0), axis=1, keepdims=True)
    slot = (mine * 8.0 + rank).astype(jnp.int32)
    at = iota((VIS, SLOTS), 1)
    order = [jnp.where(at == slot + CAP * half, 1.0, 0.0) for half in range(2)]
    order_ref[...] = jnp.concatenate(order, axis=0).astype(BF16)


def terms_kernel(order_ref, arrived_ref, unit_ref, text_ref, terms_ref, upper_ref):
    step = 8 * LANES
    for k in range(0, WIDTH, step):
        half, at = divmod(k, HALF)
        upper = dot(order_ref[half * VIS : (half + 1) * VIS, :], arrived_ref[:, at : at + step])
        upper_ref[:, k : k + step] = upper.astype(BF16)
        product = upper * unit_ref[:, k : k + step]
        total = jnp.sum(product, axis=0, keepdims=True)
        block = k // LANES
        rows = [total[:, b * LANES : (b + 1) * LANES] for b in range(8)]
        terms_ref[block : block + 8, :] = text_ref[block : block + 8, :] + jnp.concatenate(rows, axis=0)


def grads_kernel(arrived_ref, upper_ref, unit_ref, inv_ref, grad_ref):
    total = jnp.zeros((VIS, LANES), F32)
    for b in range(BLOCKS):
        at = slice(b * LANES, (b + 1) * LANES)
        gain = arrived_ref[b : b + 1, HALF:].astype(F32)
        total = total + upper_ref[:, at].astype(F32) * gain * unit_ref[:, at]
    inner = jnp.sum(total, axis=1, keepdims=True) * (1.0 / WIDTH)
    inv = inv_ref[...]
    for b in range(BLOCKS):
        at = slice(b * LANES, (b + 1) * LANES)
        gain = arrived_ref[b : b + 1, HALF:].astype(F32)
        scaled = upper_ref[:, at].astype(F32) * gain
        grad_ref[:, at] = (inv * (scaled - unit_ref[:, at] * inner)).astype(BF16)


def kernel_call(body, outs, in_specs, cost):
    return pl.pallas_call(
        body,
        out_shape=outs,
        in_specs=in_specs,
        out_specs=[VMEM] * len(outs),
        compiler_params=pltpu.CompilerParams(vmem_limit_bytes=16 * 2**20),
        cost_estimate=pl.CostEstimate(flops=cost, bytes_accessed=cost, transcendentals=0),
    )


def exchange(value, axes):
    return lax.all_to_all(value, axes, split_axis=0, concat_axis=0, tiled=True)


def turned(value, steps):
    pairs = [(source, (source + steps) % N_QUARTER) for source in range(N_QUARTER)]
    return lax.ppermute(value, QUARTER, pairs)


def shape(*dims, dtype=F32):
    return jax.ShapeDtypeStruct(dims, dtype)


def program(text, vision, vision_token, gain, cotangent):
    device = jnp.full((1,), lax.axis_index(AXES), jnp.int32)
    tokens = exchange(
        jnp.broadcast_to(vision_token[None, :], (N_QUARTER * N_FSDP, VIS)), QUARTER + FSDP
    )
    rows = turned(vision, 1)

    sent, order, taken = kernel_call(
        pack_kernel,
        [shape(SLOTS, HALF + LANES, dtype=BF16), shape(2 * VIS, SLOTS, dtype=BF16), shape(8, TOK)],
        [SMEM, VMEM, VMEM, VMEM],
        2 * 2**20,
    )(device, tokens, gain.reshape(8, LANES), cotangent)
    arrived = exchange(sent, FSDP)

    values = text.astype(F32)
    inv = lax.rsqrt(jnp.mean(values * values, axis=-1, keepdims=True) + 1e-06)
    kept = jnp.where(taken[0][:, None] > 0.0, 0.0, inv)
    text_terms = jnp.sum(cotangent.astype(F32) * values * kept, axis=0)

    values_v = rows.astype(F32)
    inv_v = lax.rsqrt(jnp.mean(values_v * values_v, axis=-1, keepdims=True) + 1e-06)
    unit = values_v * inv_v
    terms, upper = kernel_call(
        terms_kernel, [shape(BLOCKS, LANES), shape(VIS, WIDTH, dtype=BF16)], [VMEM] * 4, 2**20
    )(order, arrived, unit, text_terms.reshape(BLOCKS, LANES))
    (grad,) = kernel_call(grads_kernel, [shape(VIS, WIDTH, dtype=BF16)], [VMEM] * 4, 2**20)(
        arrived, upper, unit, jnp.broadcast_to(inv_v, (VIS, LANES))
    )
    vision_grad = turned(grad, -1)

    pieces = exchange(terms, PLANE)
    part = jnp.sum(pieces, axis=0)
    parts = exchange(jnp.broadcast_to(part[None, :], (DEVICES // N_FSDP, LANES)), GRP)
    gain_grad = jnp.sum(parts.reshape(2, 12, 4, LANES), axis=1).reshape(WIDTH // N_FSDP)
    return (vision_grad, gain_grad)


def solution(mesh):
    fine = Mesh(mesh.devices.reshape(SIZES), AXES)
    return jax.shard_map(
        program,
        mesh=fine,
        in_specs=(P(AXES, None), P(AXES, None), P(AXES), P(FSDP), P(AXES, None)),
        out_specs=(P(AXES, None), P(FSDP)),
        check_vma=False,
    )
```

```python
import jax
import jax.numpy as jnp
from jax import lax
from jax.experimental import pallas as pl
from jax.experimental.pallas import tpu as pltpu
from jax.sharding import Mesh, PartitionSpec as P

AXES = ("ylo", "zhi", "zlo", "x", "yhi", "core")
QUARTER = ("ylo", "zhi")
FSDP = ("yhi", "core")
SIZES = (2, 2, 6, 4, 4, 2)
DEVICES = 768
N_QUARTER = 4
N_FSDP = 8
CAP = 4
TOK = 128
VIS = 16
WIDTH = 8192
HALF = WIDTH // 2
LANES = 128
SLOTS = N_FSDP * 2 * CAP
BLOCKS = WIDTH // LANES
F32 = jnp.float32
BF16 = jnp.bfloat16
VMEM = pl.BlockSpec(memory_space=pltpu.VMEM)
SMEM = pl.BlockSpec(memory_space=pltpu.SMEM)


def iota(shape, dim):
    return lax.broadcasted_iota(jnp.int32, shape, dim)


def dot(a, b):
    return jnp.dot(a, b, preferred_element_type=F32)


def pack_kernel(dev_ref, tok_ref, gain_ref, cot_ref, sent_ref, order_ref, taken_ref):
    dev = dev_ref[0]
    source = lax.rem(dev // (DEVICES // N_QUARTER) + N_QUARTER - 1, N_QUARTER) * N_FSDP
    tokens = tok_ref[pl.ds(pl.multiple_of(source, N_FSDP), N_FSDP), :]
    position = dev * TOK + iota((N_FSDP, TOK), 1)
    count = jnp.zeros((N_FSDP, TOK), jnp.int32)
    chosen = [jnp.zeros((N_FSDP, TOK), F32)] * CAP
    for i in range(VIS):
        token = jnp.broadcast_to(tokens[:, i : i + 1], (N_FSDP, TOK))
        hit = token == position
        for r in range(CAP):
            chosen[r] = jnp.where(hit & (count == r), 1.0, chosen[r])
        count = count + jnp.where((token >> 7) == dev, 1, 0)
    chosen = jnp.concatenate(chosen, axis=0)
    taken_ref[...] = jnp.broadcast_to(jnp.sum(chosen, axis=0, keepdims=True), taken_ref.shape)
    chosen = chosen.astype(BF16)
    row, col = iota((SLOTS, N_FSDP * CAP), 0), iota((SLOTS, N_FSDP * CAP), 1)
    halves = []
    for half in range(2):
        at = ((col & 7) == (row >> 3)) & ((col >> 3) + CAP * half == (row & 7))
        halves.append(dot(jnp.where(at, 1.0, 0.0).astype(BF16), chosen).astype(BF16))
    lhs = jnp.concatenate(halves, axis=1)
    step = 512
    for k in range(0, HALF, step):
        rhs = jnp.concatenate([cot_ref[:, k : k + step], cot_ref[:, HALF + k : HALF + k + step]], axis=0)
        sent_ref[:, k : k + step] = dot(lhs, rhs).astype(BF16)
    gain = gain_ref[...].astype(F32)
    sent_ref[:, HALF:] = jnp.concatenate([gain] * N_FSDP, axis=0).astype(BF16)
    own = jnp.broadcast_to(tok_ref[pl.ds(source + lax.rem(dev, N_FSDP), 1), :], (VIS, VIS))
    i, j = iota((VIS, VIS), 0), iota((VIS, VIS), 1)
    target = ((own >> 7) & (N_FSDP - 1)).astype(F32)
    mine = jnp.sum(jnp.where(i == j, target, 0.0), axis=1, keepdims=True)
    rank = jnp.sum(jnp.where((target == mine) & (j < i), 1.0, 0.0), axis=1, keepdims=True)
    slot = (mine * 8.0 + rank).astype(jnp.int32)
    at = iota((VIS, SLOTS), 1)
    order = [jnp.where(at == slot + CAP * half, 1.0, 0.0) for half in range(2)]
    order_ref[...] = jnp.concatenate(order, axis=0).astype(BF16)


def terms_kernel(order_ref, arrived_ref, unit_ref, text_ref, terms_ref, upper_ref):
    step = 8 * LANES
    for k in range(0, WIDTH, step):
        half, at = divmod(k, HALF)
        upper = dot(order_ref[half * VIS : (half + 1) * VIS, :], arrived_ref[:, at : at + step])
        upper_ref[:, k : k + step] = upper.astype(BF16)
        product = upper * unit_ref[:, k : k + step]
        total = jnp.sum(product, axis=0, keepdims=True)
        block = k // LANES
        rows = [total[:, b * LANES : (b + 1) * LANES] for b in range(8)]
        terms_ref[block : block + 8, :] = text_ref[block : block + 8, :] + jnp.concatenate(rows, axis=0)


def grads_kernel(arrived_ref, upper_ref, unit_ref, inv_ref, grad_ref):
    total = jnp.zeros((VIS, LANES), F32)
    for b in range(BLOCKS):
        at = slice(b * LANES, (b + 1) * LANES)
        gain = arrived_ref[b : b + 1, HALF:].astype(F32)
        total = total + upper_ref[:, at].astype(F32) * gain * unit_ref[:, at]
    inner = jnp.sum(total, axis=1, keepdims=True) * (1.0 / WIDTH)
    inv = inv_ref[...]
    for b in range(BLOCKS):
        at = slice(b * LANES, (b + 1) * LANES)
        gain = arrived_ref[b : b + 1, HALF:].astype(F32)
        scaled = upper_ref[:, at].astype(F32) * gain
        grad_ref[:, at] = (inv * (scaled - unit_ref[:, at] * inner)).astype(BF16)


def copy_kernel(in_ref, out_ref):
    out_ref[...] = in_ref[...]


def kernel_call(body, outs, in_specs, cost):
    return pl.pallas_call(
        body,
        out_shape=outs,
        in_specs=in_specs,
        out_specs=[VMEM] * len(outs),
        compiler_params=pltpu.CompilerParams(vmem_limit_bytes=16 * 2**20),
        cost_estimate=pl.CostEstimate(flops=cost, bytes_accessed=cost, transcendentals=0),
    )


def exchange(value, axes):
    return lax.all_to_all(value, axes, split_axis=0, concat_axis=0, tiled=True)


def turned(value, steps):
    pairs = [(source, (source + steps) % N_QUARTER) for source in range(N_QUARTER)]
    return lax.ppermute(value, QUARTER, pairs)


def repeated(part, times):
    return jnp.broadcast_to(part[None], (times, 8, LANES)).reshape(times * 8, LANES)


def added(pieces):
    return jnp.sum(pieces.reshape(-1, 8, LANES), axis=0)


def shape(*dims, dtype=F32):
    return jax.ShapeDtypeStruct(dims, dtype)


def program(text, vision, vision_token, gain, cotangent):
    device = jnp.full((1,), lax.axis_index(AXES), jnp.int32)
    tokens = exchange(
        jnp.broadcast_to(vision_token[None, :], (N_QUARTER * N_FSDP, VIS)), QUARTER + FSDP
    )
    rows = turned(vision, 1)

    sent, order, taken = kernel_call(
        pack_kernel,
        [shape(SLOTS, HALF + LANES, dtype=BF16), shape(2 * VIS, SLOTS, dtype=BF16), shape(8, TOK)],
        [SMEM, VMEM, VMEM, VMEM],
        2 * 2**20,
    )(device, tokens, gain.reshape(8, LANES), cotangent)
    arrived = exchange(sent, FSDP)

    values = text.astype(F32)
    inv = lax.rsqrt(jnp.mean(values * values, axis=-1, keepdims=True) + 1e-06)
    kept = jnp.where(taken[0][:, None] > 0.0, 0.0, inv)
    text_terms = jnp.sum(cotangent.astype(F32) * values * kept, axis=0)

    values_v = rows.astype(F32)
    inv_v = lax.rsqrt(jnp.mean(values_v * values_v, axis=-1, keepdims=True) + 1e-06)
    unit = values_v * inv_v
    terms, upper = kernel_call(
        terms_kernel, [shape(BLOCKS, LANES), shape(VIS, WIDTH, dtype=BF16)], [VMEM] * 4, 2**20
    )(order, arrived, unit, text_terms.reshape(BLOCKS, LANES))
    (grad,) = kernel_call(grads_kernel, [shape(VIS, WIDTH, dtype=BF16)], [VMEM] * 4, 2**20)(
        arrived, upper, unit, jnp.broadcast_to(inv_v, (VIS, LANES))
    )
    vision_grad = turned(grad, -1)

    (vision_grad,) = kernel_call(copy_kernel, [shape(VIS, WIDTH, dtype=BF16)], [VMEM], 2**18)(
        vision_grad
    )

    part = added(exchange(terms, FSDP))
    part = added(exchange(repeated(part, 8), ("ylo", "x")))
    part = added(exchange(repeated(part, 12), ("zhi", "zlo")))
    return (vision_grad, part.reshape(WIDTH // N_FSDP))


def solution(mesh):
    fine = Mesh(mesh.devices.reshape(SIZES), AXES)
    return jax.shard_map(
        program,
        mesh=fine,
        in_specs=(P(AXES, None), P(AXES, None), P(AXES), P(FSDP), P(AXES, None)),
        out_specs=(P(AXES, None), P(FSDP)),
        check_vma=False,
    )
```

```python
import jax
import jax.numpy as jnp
from jax import lax
from jax.experimental import pallas as pl
from jax.experimental.pallas import tpu as pltpu
from jax.sharding import Mesh, PartitionSpec as P

AXES = ("ylo", "zhi", "zlo", "x", "yhi", "core")
QUARTER = ("ylo", "zhi")
FSDP = ("yhi", "core")
SIZES = (2, 2, 6, 4, 4, 2)
DEVICES = 768
N_QUARTER = 4
N_FSDP = 8
CAP = 4
TOK = 128
VIS = 16
WIDTH = 8192
HALF = WIDTH // 2
LANES = 128
SLOTS = N_FSDP * 2 * CAP
BLOCKS = WIDTH // LANES
FIRST = 6144
F32 = jnp.float32
BF16 = jnp.bfloat16
VMEM = pl.BlockSpec(memory_space=pltpu.VMEM)
SMEM = pl.BlockSpec(memory_space=pltpu.SMEM)


def iota(shape, dim):
    return lax.broadcasted_iota(jnp.int32, shape, dim)


def dot(a, b):
    return jnp.dot(a, b, preferred_element_type=F32)


def pack_kernel(dev_ref, tok_ref, gain_ref, cot_ref, sent_ref, order_ref, taken_ref):
    dev = dev_ref[0]
    source = lax.rem(dev // (DEVICES // N_QUARTER) + N_QUARTER - 1, N_QUARTER) * N_FSDP
    tokens = tok_ref[pl.ds(pl.multiple_of(source, N_FSDP), N_FSDP), :]
    position = dev * TOK + iota((N_FSDP, TOK), 1)
    count = jnp.zeros((N_FSDP, TOK), jnp.int32)
    chosen = [jnp.zeros((N_FSDP, TOK), F32)] * CAP
    for i in range(VIS):
        token = jnp.broadcast_to(tokens[:, i : i + 1], (N_FSDP, TOK))
        hit = token == position
        for r in range(CAP):
            chosen[r] = jnp.where(hit & (count == r), 1.0, chosen[r])
        count = count + jnp.where((token >> 7) == dev, 1, 0)
    chosen = jnp.concatenate(chosen, axis=0)
    taken_ref[...] = jnp.broadcast_to(jnp.sum(chosen, axis=0, keepdims=True), taken_ref.shape)
    chosen = chosen.astype(BF16)
    row, col = iota((SLOTS, N_FSDP * CAP), 0), iota((SLOTS, N_FSDP * CAP), 1)
    halves = []
    for half in range(2):
        at = ((col & 7) == (row >> 3)) & ((col >> 3) + CAP * half == (row & 7))
        halves.append(dot(jnp.where(at, 1.0, 0.0).astype(BF16), chosen).astype(BF16))
    lhs = jnp.concatenate(halves, axis=1)
    step = 512
    for k in range(0, HALF, step):
        rhs = jnp.concatenate([cot_ref[:, k : k + step], cot_ref[:, HALF + k : HALF + k + step]], axis=0)
        sent_ref[:, k : k + step] = dot(lhs, rhs).astype(BF16)
    gain = gain_ref[...].astype(F32)
    sent_ref[:, HALF:] = jnp.concatenate([gain] * N_FSDP, axis=0).astype(BF16)
    own = jnp.broadcast_to(tok_ref[pl.ds(source + lax.rem(dev, N_FSDP), 1), :], (VIS, VIS))
    i, j = iota((VIS, VIS), 0), iota((VIS, VIS), 1)
    target = ((own >> 7) & (N_FSDP - 1)).astype(F32)
    mine = jnp.sum(jnp.where(i == j, target, 0.0), axis=1, keepdims=True)
    rank = jnp.sum(jnp.where((target == mine) & (j < i), 1.0, 0.0), axis=1, keepdims=True)
    slot = (mine * 8.0 + rank).astype(jnp.int32)
    at = iota((VIS, SLOTS), 1)
    order = [jnp.where(at == slot + CAP * half, 1.0, 0.0) for half in range(2)]
    order_ref[...] = jnp.concatenate(order, axis=0).astype(BF16)


def terms_kernel(order_ref, arrived_ref, unit_ref, text_ref, terms_ref, upper_ref):
    step = 8 * LANES
    for k in range(0, WIDTH, step):
        half, at = divmod(k, HALF)
        upper = dot(order_ref[half * VIS : (half + 1) * VIS, :], arrived_ref[:, at : at + step])
        upper_ref[:, k : k + step] = upper.astype(BF16)
        product = upper * unit_ref[:, k : k + step]
        total = jnp.sum(product, axis=0, keepdims=True)
        block = k // LANES
        rows = [total[:, b * LANES : (b + 1) * LANES] for b in range(8)]
        terms_ref[block : block + 8, :] = text_ref[block : block + 8, :] + jnp.concatenate(rows, axis=0)


def grads_kernel(arrived_ref, upper_ref, unit_ref, inv_ref, first_ref, last_ref):
    total = jnp.zeros((VIS, LANES), F32)
    for b in range(BLOCKS):
        at = slice(b * LANES, (b + 1) * LANES)
        gain = arrived_ref[b : b + 1, HALF:].astype(F32)
        total = total + upper_ref[:, at].astype(F32) * gain * unit_ref[:, at]
    inner = jnp.sum(total, axis=1, keepdims=True) * (1.0 / WIDTH)
    inv = inv_ref[...]
    for b in range(BLOCKS):
        at = slice(b * LANES, (b + 1) * LANES)
        gain = arrived_ref[b : b + 1, HALF:].astype(F32)
        scaled = upper_ref[:, at].astype(F32) * gain
        grad = (inv * (scaled - unit_ref[:, at] * inner)).astype(BF16)
        if b * LANES < FIRST:
            first_ref[:, at] = grad
        else:
            last_ref[:, b * LANES - FIRST : (b + 1) * LANES - FIRST] = grad


def repeat_kernel(tok_ref, out_ref):
    out_ref[...] = jnp.broadcast_to(tok_ref[...], out_ref.shape)


def finish_kernel(pieces_ref, first_ref, last_ref, grad_ref, sum_ref):
    grad_ref[:, :FIRST] = first_ref[...]
    grad_ref[:, FIRST:] = last_ref[...]
    total = pieces_ref[:8, :]
    for k in range(1, 12):
        total = total + pieces_ref[8 * k : 8 * k + 8, :]
    sum_ref[...] = total


def kernel_call(body, outs, in_specs, cost):
    return pl.pallas_call(
        body,
        out_shape=outs,
        in_specs=in_specs,
        out_specs=[VMEM] * len(outs),
        compiler_params=pltpu.CompilerParams(vmem_limit_bytes=16 * 2**20),
        cost_estimate=pl.CostEstimate(flops=cost, bytes_accessed=cost, transcendentals=0),
    )


def exchange(value, axes):
    return lax.all_to_all(value, axes, split_axis=0, concat_axis=0, tiled=True)


def turned(value, steps):
    pairs = [(source, (source + steps) % N_QUARTER) for source in range(N_QUARTER)]
    return lax.ppermute(value, QUARTER, pairs)


def repeated(part, times):
    return jnp.broadcast_to(part[None], (times, 8, LANES)).reshape(times * 8, LANES)


def added(pieces):
    return jnp.sum(pieces.reshape(-1, 8, LANES), axis=0)


def shape(*dims, dtype=F32):
    return jax.ShapeDtypeStruct(dims, dtype)


def program(text, vision, vision_token, gain, cotangent):
    device = jnp.full((1,), lax.axis_index(AXES), jnp.int32)
    (asked,) = kernel_call(
        repeat_kernel, [shape(N_QUARTER * N_FSDP, VIS, dtype=jnp.int32)], [VMEM], 2**12
    )(vision_token.reshape(1, VIS))
    tokens = exchange(asked, QUARTER + FSDP)
    rows = turned(vision, 1)

    sent, order, taken = kernel_call(
        pack_kernel,
        [shape(SLOTS, HALF + LANES, dtype=BF16), shape(2 * VIS, SLOTS, dtype=BF16), shape(8, TOK)],
        [SMEM, VMEM, VMEM, VMEM],
        2 * 2**20,
    )(device, tokens, gain.reshape(8, LANES), cotangent)
    arrived = exchange(sent, FSDP)

    values = text.astype(F32)
    inv = lax.rsqrt(jnp.mean(values * values, axis=-1, keepdims=True) + 1e-06)
    kept = jnp.where(taken[0][:, None] > 0.0, 0.0, inv)
    text_terms = jnp.sum(cotangent.astype(F32) * values * kept, axis=0)

    values_v = rows.astype(F32)
    inv_v = lax.rsqrt(jnp.mean(values_v * values_v, axis=-1, keepdims=True) + 1e-06)
    unit = values_v * inv_v
    terms, upper = kernel_call(
        terms_kernel, [shape(BLOCKS, LANES), shape(VIS, WIDTH, dtype=BF16)], [VMEM] * 4, 2**20
    )(order, arrived, unit, text_terms.reshape(BLOCKS, LANES))
    first, last = kernel_call(
        grads_kernel,
        [shape(VIS, FIRST, dtype=BF16), shape(VIS, WIDTH - FIRST, dtype=BF16)],
        [VMEM] * 4,
        2**20,
    )(arrived, upper, unit, jnp.broadcast_to(inv_v, (VIS, LANES)))
    first = turned(first, -1)
    last = turned(last, -1)

    part = added(exchange(terms, FSDP))
    part = added(exchange(repeated(part, 8), ("ylo", "x")))
    pieces = exchange(repeated(part, 12), ("zhi", "zlo"))
    vision_grad, gain_grad = kernel_call(
        finish_kernel, [shape(VIS, WIDTH, dtype=BF16), shape(8, LANES)], [VMEM] * 3, 2**19
    )(pieces, first, last)
    return (vision_grad, gain_grad.reshape(WIDTH // N_FSDP))


def solution(mesh):
    fine = Mesh(mesh.devices.reshape(SIZES), AXES)
    return jax.shard_map(
        program,
        mesh=fine,
        in_specs=(P(AXES, None), P(AXES, None), P(AXES), P(FSDP), P(AXES, None)),
        out_specs=(P(AXES, None), P(FSDP)),
        check_vma=False,
    )
```

```python
import jax
import jax.numpy as jnp
from jax import lax
from jax.experimental import pallas as pl
from jax.experimental.pallas import tpu as pltpu
from jax.sharding import Mesh, PartitionSpec as P

AXES = ("ylo", "zhi", "zlo", "x", "yhi", "core")
QUARTER = ("ylo", "zhi")
GRP = ("ylo", "zhi", "zlo", "x")
FSDP = ("yhi", "core")
PLANE = ("yhi", "core", "ylo", "x")
SIZES = (2, 2, 6, 4, 4, 2)
DEVICES = 768
N_QUARTER = 4
N_FSDP = 8
CAP = 4
TOK = 128
VIS = 16
WIDTH = 8192
HALF = WIDTH // 2
LANES = 128
SLOTS = N_FSDP * 2 * CAP
BLOCKS = WIDTH // LANES
F32 = jnp.float32
BF16 = jnp.bfloat16
VMEM = pl.BlockSpec(memory_space=pltpu.VMEM)
SMEM = pl.BlockSpec(memory_space=pltpu.SMEM)


def iota(shape, dim):
    return lax.broadcasted_iota(jnp.int32, shape, dim)


def dot(a, b):
    return jnp.dot(a, b, preferred_element_type=F32)


def pack_kernel(dev_ref, tok_ref, gain_ref, cot_ref, sent_ref, order_ref, taken_ref):
    dev = dev_ref[0]
    source = lax.rem(dev // (DEVICES // N_QUARTER) + N_QUARTER - 1, N_QUARTER) * N_FSDP
    tokens = tok_ref[pl.ds(pl.multiple_of(source, N_FSDP), N_FSDP), :]
    position = dev * TOK + iota((N_FSDP, TOK), 1)
    count = jnp.zeros((N_FSDP, TOK), jnp.int32)
    chosen = [jnp.zeros((N_FSDP, TOK), F32)] * CAP
    for i in range(VIS):
        token = jnp.broadcast_to(tokens[:, i : i + 1], (N_FSDP, TOK))
        hit = token == position
        for r in range(CAP):
            chosen[r] = jnp.where(hit & (count == r), 1.0, chosen[r])
        count = count + jnp.where((token >> 7) == dev, 1, 0)
    chosen = jnp.concatenate(chosen, axis=0)
    taken_ref[...] = jnp.broadcast_to(jnp.sum(chosen, axis=0, keepdims=True), taken_ref.shape)
    chosen = chosen.astype(BF16)
    row, col = iota((SLOTS, N_FSDP * CAP), 0), iota((SLOTS, N_FSDP * CAP), 1)
    halves = []
    for half in range(2):
        at = ((col & 7) == (row >> 3)) & ((col >> 3) + CAP * half == (row & 7))
        halves.append(dot(jnp.where(at, 1.0, 0.0).astype(BF16), chosen).astype(BF16))
    lhs = jnp.concatenate(halves, axis=1)
    step = 512
    for k in range(0, HALF, step):
        rhs = jnp.concatenate([cot_ref[:, k : k + step], cot_ref[:, HALF + k : HALF + k + step]], axis=0)
        sent_ref[:, k : k + step] = dot(lhs, rhs).astype(BF16)
    gain = gain_ref[...].astype(F32)
    sent_ref[:, HALF:] = jnp.concatenate([gain] * N_FSDP, axis=0).astype(BF16)
    own = jnp.broadcast_to(tok_ref[pl.ds(source + lax.rem(dev, N_FSDP), 1), :], (VIS, VIS))
    i, j = iota((VIS, VIS), 0), iota((VIS, VIS), 1)
    target = ((own >> 7) & (N_FSDP - 1)).astype(F32)
    mine = jnp.sum(jnp.where(i == j, target, 0.0), axis=1, keepdims=True)
    rank = jnp.sum(jnp.where((target == mine) & (j < i), 1.0, 0.0), axis=1, keepdims=True)
    slot = (mine * 8.0 + rank).astype(jnp.int32)
    at = iota((VIS, SLOTS), 1)
    order = [jnp.where(at == slot + CAP * half, 1.0, 0.0) for half in range(2)]
    order_ref[...] = jnp.concatenate(order, axis=0).astype(BF16)


def terms_kernel(order_ref, arrived_ref, unit_ref, text_ref, terms_ref, upper_ref):
    step = 8 * LANES
    for k in range(0, WIDTH, step):
        half, at = divmod(k, HALF)
        upper = dot(order_ref[half * VIS : (half + 1) * VIS, :], arrived_ref[:, at : at + step])
        upper_ref[:, k : k + step] = upper.astype(BF16)
        product = upper * unit_ref[:, k : k + step]
        total = jnp.sum(product, axis=0, keepdims=True)
        block = k // LANES
        rows = [total[:, b * LANES : (b + 1) * LANES] for b in range(8)]
        terms_ref[block : block + 8, :] = text_ref[block : block + 8, :] + jnp.concatenate(rows, axis=0)


def grads_kernel(arrived_ref, upper_ref, unit_ref, inv_ref, grad_ref):
    total = jnp.zeros((VIS, LANES), F32)
    for b in range(BLOCKS):
        at = slice(b * LANES, (b + 1) * LANES)
        gain = arrived_ref[b : b + 1, HALF:].astype(F32)
        total = total + upper_ref[:, at].astype(F32) * gain * unit_ref[:, at]
    inner = jnp.sum(total, axis=1, keepdims=True) * (1.0 / WIDTH)
    inv = inv_ref[...]
    for b in range(BLOCKS):
        at = slice(b * LANES, (b + 1) * LANES)
        gain = arrived_ref[b : b + 1, HALF:].astype(F32)
        scaled = upper_ref[:, at].astype(F32) * gain
        grad_ref[:, at] = (inv * (scaled - unit_ref[:, at] * inner)).astype(BF16)


def finish_kernel(parts_ref, rows_ref, grad_ref, sum_ref):
    grad_ref[...] = rows_ref[...]
    for low in range(2):
        total = parts_ref[low * 48 : low * 48 + 4, :]
        for z in range(1, 12):
            total = total + parts_ref[low * 48 + 4 * z : low * 48 + 4 * z + 4, :]
        sum_ref[4 * low : 4 * low + 4, :] = total


def kernel_call(body, outs, in_specs, cost):
    return pl.pallas_call(
        body,
        out_shape=outs,
        in_specs=in_specs,
        out_specs=[VMEM] * len(outs),
        compiler_params=pltpu.CompilerParams(vmem_limit_bytes=16 * 2**20),
        cost_estimate=pl.CostEstimate(flops=cost, bytes_accessed=cost, transcendentals=0),
    )


def exchange(value, axes):
    return lax.all_to_all(value, axes, split_axis=0, concat_axis=0, tiled=True)


def turned(value, steps):
    pairs = [(source, (source + steps) % N_QUARTER) for source in range(N_QUARTER)]
    return lax.ppermute(value, QUARTER, pairs)


def shape(*dims, dtype=F32):
    return jax.ShapeDtypeStruct(dims, dtype)


def program(text, vision, vision_token, gain, cotangent):
    device = jnp.full((1,), lax.axis_index(AXES), jnp.int32)
    tokens = exchange(
        jnp.broadcast_to(vision_token[None, :], (N_QUARTER * N_FSDP, VIS)), QUARTER + FSDP
    )
    rows = turned(vision, 1)

    sent, order, taken = kernel_call(
        pack_kernel,
        [shape(SLOTS, HALF + LANES, dtype=BF16), shape(2 * VIS, SLOTS, dtype=BF16), shape(8, TOK)],
        [SMEM, VMEM, VMEM, VMEM],
        2 * 2**20,
    )(device, tokens, gain.reshape(8, LANES), cotangent)
    arrived = exchange(sent, FSDP)

    values = text.astype(F32)
    inv = lax.rsqrt(jnp.mean(values * values, axis=-1, keepdims=True) + 1e-06)
    kept = jnp.where(taken[0][:, None] > 0.0, 0.0, inv)
    text_terms = jnp.sum(cotangent.astype(F32) * values * kept, axis=0)

    values_v = rows.astype(F32)
    inv_v = lax.rsqrt(jnp.mean(values_v * values_v, axis=-1, keepdims=True) + 1e-06)
    unit = values_v * inv_v
    terms, upper = kernel_call(
        terms_kernel, [shape(BLOCKS, LANES), shape(VIS, WIDTH, dtype=BF16)], [VMEM] * 4, 2**20
    )(order, arrived, unit, text_terms.reshape(BLOCKS, LANES))
    (grad,) = kernel_call(grads_kernel, [shape(VIS, WIDTH, dtype=BF16)], [VMEM] * 4, 2**20)(
        arrived, upper, unit, jnp.broadcast_to(inv_v, (VIS, LANES))
    )
    vision_grad = turned(grad, -1)

    pieces = exchange(terms, PLANE)
    part = jnp.sum(pieces, axis=0)
    parts = exchange(jnp.broadcast_to(part[None, :], (DEVICES // N_FSDP, LANES)), GRP)
    vision_grad, gain_grad = kernel_call(
        finish_kernel, [shape(VIS, WIDTH, dtype=BF16), shape(8, LANES)], [VMEM] * 2, 2**19
    )(parts, vision_grad)
    return (vision_grad, gain_grad.reshape(WIDTH // N_FSDP))


def solution(mesh):
    fine = Mesh(mesh.devices.reshape(SIZES), AXES)
    return jax.shard_map(
        program,
        mesh=fine,
        in_specs=(P(AXES, None), P(AXES, None), P(AXES), P(FSDP), P(AXES, None)),
        out_specs=(P(AXES, None), P(FSDP)),
        check_vma=False,
    )
```

```python
import jax
import jax.numpy as jnp
from jax import lax
from jax.experimental import pallas as pl
from jax.experimental.pallas import tpu as pltpu
from jax.sharding import Mesh, PartitionSpec as P

AXES = ("ylo", "zhi", "zlo", "x", "yhi", "core")
QUARTER = ("ylo", "zhi")
GRP = ("ylo", "zhi", "zlo", "x")
FSDP = ("yhi", "core")
PLANE = ("yhi", "core", "ylo", "x")
SIZES = (2, 2, 6, 4, 4, 2)
DEVICES = 768
N_QUARTER = 4
N_FSDP = 8
CAP = 4
TOK = 128
VIS = 16
WIDTH = 8192
HALF = WIDTH // 2
LANES = 128
SLOTS = N_FSDP * 2 * CAP
BLOCKS = WIDTH // LANES
F32 = jnp.float32
BF16 = jnp.bfloat16
VMEM = pl.BlockSpec(memory_space=pltpu.VMEM)
SMEM = pl.BlockSpec(memory_space=pltpu.SMEM)


def iota(shape, dim):
    return lax.broadcasted_iota(jnp.int32, shape, dim)


def dot(a, b):
    return jnp.dot(a, b, preferred_element_type=F32)


def pack_kernel(dev_ref, tok_ref, gain_ref, cot_ref, sent_ref, order_ref, taken_ref):
    dev = dev_ref[0]
    tokens = tok_ref[...]
    position = dev * TOK + iota((N_FSDP, TOK), 1)
    count = jnp.zeros((N_FSDP, TOK), jnp.int32)
    chosen = [jnp.zeros((N_FSDP, TOK), F32)] * CAP
    for i in range(VIS):
        token = jnp.broadcast_to(tokens[:, i : i + 1], (N_FSDP, TOK))
        hit = token == position
        for r in range(CAP):
            chosen[r] = jnp.where(hit & (count == r), 1.0, chosen[r])
        count = count + jnp.where((token >> 7) == dev, 1, 0)
    chosen = jnp.concatenate(chosen, axis=0)
    taken_ref[...] = jnp.broadcast_to(jnp.sum(chosen, axis=0, keepdims=True), taken_ref.shape)
    chosen = chosen.astype(BF16)
    row, col = iota((SLOTS, N_FSDP * CAP), 0), iota((SLOTS, N_FSDP * CAP), 1)
    halves = []
    for half in range(2):
        at = ((col & 7) == (row >> 3)) & ((col >> 3) + CAP * half == (row & 7))
        halves.append(dot(jnp.where(at, 1.0, 0.0).astype(BF16), chosen).astype(BF16))
    lhs = jnp.concatenate(halves, axis=1)
    step = 512
    for k in range(0, HALF, step):
        rhs = jnp.concatenate([cot_ref[:, k : k + step], cot_ref[:, HALF + k : HALF + k + step]], axis=0)
        sent_ref[:, k : k + step] = dot(lhs, rhs).astype(BF16)
    gain = gain_ref[...].astype(F32)
    sent_ref[:, HALF:] = jnp.concatenate([gain] * N_FSDP, axis=0).astype(BF16)
    own = jnp.broadcast_to(tok_ref[pl.ds(lax.rem(dev, N_FSDP), 1), :], (VIS, VIS))
    i, j = iota((VIS, VIS), 0), iota((VIS, VIS), 1)
    target = ((own >> 7) & (N_FSDP - 1)).astype(F32)
    mine = jnp.sum(jnp.where(i == j, target, 0.0), axis=1, keepdims=True)
    rank = jnp.sum(jnp.where((target == mine) & (j < i), 1.0, 0.0), axis=1, keepdims=True)
    slot = (mine * 8.0 + rank).astype(jnp.int32)
    at = iota((VIS, SLOTS), 1)
    order = [jnp.where(at == slot + CAP * half, 1.0, 0.0) for half in range(2)]
    order_ref[...] = jnp.concatenate(order, axis=0).astype(BF16)


def terms_kernel(order_ref, arrived_ref, unit_ref, text_ref, terms_ref, upper_ref):
    step = 8 * LANES
    for k in range(0, WIDTH, step):
        half, at = divmod(k, HALF)
        upper = dot(order_ref[half * VIS : (half + 1) * VIS, :], arrived_ref[:, at : at + step])
        upper_ref[:, k : k + step] = upper.astype(BF16)
        product = upper * unit_ref[:, k : k + step]
        total = jnp.sum(product, axis=0, keepdims=True)
        block = k // LANES
        rows = [total[:, b * LANES : (b + 1) * LANES] for b in range(8)]
        terms_ref[block : block + 8, :] = text_ref[block : block + 8, :] + jnp.concatenate(rows, axis=0)


def grads_kernel(arrived_ref, upper_ref, unit_ref, inv_ref, grad_ref):
    total = jnp.zeros((VIS, LANES), F32)
    for b in range(BLOCKS):
        at = slice(b * LANES, (b + 1) * LANES)
        gain = arrived_ref[b : b + 1, HALF:].astype(F32)
        total = total + upper_ref[:, at].astype(F32) * gain * unit_ref[:, at]
    inner = jnp.sum(total, axis=1, keepdims=True) * (1.0 / WIDTH)
    inv = inv_ref[...]
    for b in range(BLOCKS):
        at = slice(b * LANES, (b + 1) * LANES)
        gain = arrived_ref[b : b + 1, HALF:].astype(F32)
        scaled = upper_ref[:, at].astype(F32) * gain
        grad_ref[:, at] = (inv * (scaled - unit_ref[:, at] * inner)).astype(BF16)


def finish_kernel(parts_ref, rows_ref, grad_ref, sum_ref):
    grad_ref[...] = rows_ref[...]
    for low in range(2):
        total = parts_ref[low * 48 : low * 48 + 4, :]
        for z in range(1, 12):
            total = total + parts_ref[low * 48 + 4 * z : low * 48 + 4 * z + 4, :]
        sum_ref[4 * low : 4 * low + 4, :] = total


def kernel_call(body, outs, in_specs, cost):
    return pl.pallas_call(
        body,
        out_shape=outs,
        in_specs=in_specs,
        out_specs=[VMEM] * len(outs),
        compiler_params=pltpu.CompilerParams(vmem_limit_bytes=16 * 2**20),
        cost_estimate=pl.CostEstimate(flops=cost, bytes_accessed=cost, transcendentals=0),
    )


def exchange(value, axes):
    return lax.all_to_all(value, axes, split_axis=0, concat_axis=0, tiled=True)


def turned(value, steps):
    pairs = [(source, (source + steps) % N_QUARTER) for source in range(N_QUARTER)]
    return lax.ppermute(value, QUARTER, pairs)


def shape(*dims, dtype=F32):
    return jax.ShapeDtypeStruct(dims, dtype)


def program(text, vision, vision_token, gain, cotangent):
    device = jnp.full((1,), lax.axis_index(AXES), jnp.int32)
    asked = turned(jnp.broadcast_to(vision_token[None, :], (N_FSDP, VIS)), 1)
    rows = turned(vision, 1)
    tokens = exchange(asked, FSDP)

    sent, order, taken = kernel_call(
        pack_kernel,
        [shape(SLOTS, HALF + LANES, dtype=BF16), shape(2 * VIS, SLOTS, dtype=BF16), shape(8, TOK)],
        [SMEM, VMEM, VMEM, VMEM],
        2 * 2**20,
    )(device, tokens, gain.reshape(8, LANES), cotangent)
    arrived = exchange(sent, FSDP)

    values = text.astype(F32)
    inv = lax.rsqrt(jnp.mean(values * values, axis=-1, keepdims=True) + 1e-06)
    kept = jnp.where(taken[0][:, None] > 0.0, 0.0, inv)
    text_terms = jnp.sum(cotangent.astype(F32) * values * kept, axis=0)

    values_v = rows.astype(F32)
    inv_v = lax.rsqrt(jnp.mean(values_v * values_v, axis=-1, keepdims=True) + 1e-06)
    unit = values_v * inv_v
    terms, upper = kernel_call(
        terms_kernel, [shape(BLOCKS, LANES), shape(VIS, WIDTH, dtype=BF16)], [VMEM] * 4, 2**20
    )(order, arrived, unit, text_terms.reshape(BLOCKS, LANES))
    (grad,) = kernel_call(grads_kernel, [shape(VIS, WIDTH, dtype=BF16)], [VMEM] * 4, 2**20)(
        arrived, upper, unit, jnp.broadcast_to(inv_v, (VIS, LANES))
    )
    vision_grad = turned(grad, -1)

    pieces = exchange(terms, PLANE)
    part = jnp.sum(pieces, axis=0)
    parts = exchange(jnp.broadcast_to(part[None, :], (DEVICES // N_FSDP, LANES)), GRP)
    vision_grad, gain_grad = kernel_call(
        finish_kernel, [shape(VIS, WIDTH, dtype=BF16), shape(8, LANES)], [VMEM] * 2, 2**19
    )(parts, vision_grad)
    return (vision_grad, gain_grad.reshape(WIDTH // N_FSDP))


def solution(mesh):
    fine = Mesh(mesh.devices.reshape(SIZES), AXES)
    return jax.shard_map(
        program,
        mesh=fine,
        in_specs=(P(AXES, None), P(AXES, None), P(AXES), P(FSDP), P(AXES, None)),
        out_specs=(P(AXES, None), P(FSDP)),
        check_vma=False,
    )
```

```python
import jax
import jax.numpy as jnp
from jax import lax
from jax.experimental import pallas as pl
from jax.experimental.pallas import tpu as pltpu
from jax.sharding import Mesh, PartitionSpec as P

AXES = ("ylo", "zhi", "zlo", "x", "yhi", "core")
QUARTER = ("ylo", "zhi")
ZX = ("zhi", "zlo", "x")
FSDP = ("yhi", "core")
PLANE = ("yhi", "core", "ylo", "x")
SIZES = (2, 2, 6, 4, 4, 2)
DEVICES = 768
N_QUARTER = 4
N_FSDP = 8
CAP = 4
TOK = 128
VIS = 16
WIDTH = 8192
HALF = WIDTH // 2
LANES = 128
SLOTS = N_FSDP * 2 * CAP
BLOCKS = WIDTH // LANES
F32 = jnp.float32
BF16 = jnp.bfloat16
VMEM = pl.BlockSpec(memory_space=pltpu.VMEM)
SMEM = pl.BlockSpec(memory_space=pltpu.SMEM)


def iota(shape, dim):
    return lax.broadcasted_iota(jnp.int32, shape, dim)


def dot(a, b):
    return jnp.dot(a, b, preferred_element_type=F32)


def pack_kernel(dev_ref, tok_ref, gain_ref, cot_ref, sent_ref, order_ref, taken_ref):
    dev = dev_ref[0]
    source = lax.rem(dev // (DEVICES // N_QUARTER) + N_QUARTER - 1, N_QUARTER) * N_FSDP
    tokens = tok_ref[pl.ds(pl.multiple_of(source, N_FSDP), N_FSDP), :]
    position = dev * TOK + iota((N_FSDP, TOK), 1)
    count = jnp.zeros((N_FSDP, TOK), jnp.int32)
    chosen = [jnp.zeros((N_FSDP, TOK), F32)] * CAP
    for i in range(VIS):
        token = jnp.broadcast_to(tokens[:, i : i + 1], (N_FSDP, TOK))
        hit = token == position
        for r in range(CAP):
            chosen[r] = jnp.where(hit & (count == r), 1.0, chosen[r])
        count = count + jnp.where((token >> 7) == dev, 1, 0)
    chosen = jnp.concatenate(chosen, axis=0)
    taken_ref[...] = jnp.broadcast_to(jnp.sum(chosen, axis=0, keepdims=True), taken_ref.shape)
    chosen = chosen.astype(BF16)
    row, col = iota((SLOTS, N_FSDP * CAP), 0), iota((SLOTS, N_FSDP * CAP), 1)
    halves = []
    for half in range(2):
        at = ((col & 7) == (row >> 3)) & ((col >> 3) + CAP * half == (row & 7))
        halves.append(dot(jnp.where(at, 1.0, 0.0).astype(BF16), chosen).astype(BF16))
    lhs = jnp.concatenate(halves, axis=1)
    step = 512
    for k in range(0, HALF, step):
        rhs = jnp.concatenate([cot_ref[:, k : k + step], cot_ref[:, HALF + k : HALF + k + step]], axis=0)
        sent_ref[:, k : k + step] = dot(lhs, rhs).astype(BF16)
    gain = gain_ref[...].astype(F32)
    sent_ref[:, HALF:] = jnp.concatenate([gain] * N_FSDP, axis=0).astype(BF16)
    own = jnp.broadcast_to(tok_ref[pl.ds(source + lax.rem(dev, N_FSDP), 1), :], (VIS, VIS))
    i, j = iota((VIS, VIS), 0), iota((VIS, VIS), 1)
    target = ((own >> 7) & (N_FSDP - 1)).astype(F32)
    mine = jnp.sum(jnp.where(i == j, target, 0.0), axis=1, keepdims=True)
    rank = jnp.sum(jnp.where((target == mine) & (j < i), 1.0, 0.0), axis=1, keepdims=True)
    slot = (mine * 8.0 + rank).astype(jnp.int32)
    at = iota((VIS, SLOTS), 1)
    order = [jnp.where(at == slot + CAP * half, 1.0, 0.0) for half in range(2)]
    order_ref[...] = jnp.concatenate(order, axis=0).astype(BF16)


def terms_kernel(order_ref, arrived_ref, unit_ref, text_ref, terms_ref, upper_ref):
    step = 8 * LANES
    for k in range(0, WIDTH, step):
        half, at = divmod(k, HALF)
        upper = dot(order_ref[half * VIS : (half + 1) * VIS, :], arrived_ref[:, at : at + step])
        upper_ref[:, k : k + step] = upper.astype(BF16)
        product = upper * unit_ref[:, k : k + step]
        total = jnp.sum(product, axis=0, keepdims=True)
        block = k // LANES
        rows = [total[:, b * LANES : (b + 1) * LANES] for b in range(8)]
        rows = text_ref[block : block + 8, :] + jnp.concatenate(rows, axis=0)
        terms_ref[2 * block : 2 * block + 8, :] = rows
        terms_ref[2 * block + 8 : 2 * block + 16, :] = rows


def grads_kernel(arrived_ref, upper_ref, unit_ref, inv_ref, grad_ref):
    total = jnp.zeros((VIS, LANES), F32)
    for b in range(BLOCKS):
        at = slice(b * LANES, (b + 1) * LANES)
        gain = arrived_ref[b : b + 1, HALF:].astype(F32)
        total = total + upper_ref[:, at].astype(F32) * gain * unit_ref[:, at]
    inner = jnp.sum(total, axis=1, keepdims=True) * (1.0 / WIDTH)
    inv = inv_ref[...]
    for b in range(BLOCKS):
        at = slice(b * LANES, (b + 1) * LANES)
        gain = arrived_ref[b : b + 1, HALF:].astype(F32)
        scaled = upper_ref[:, at].astype(F32) * gain
        grad_ref[:, at] = (inv * (scaled - unit_ref[:, at] * inner)).astype(BF16)


def finish_kernel(parts_ref, rows_ref, grad_ref, sum_ref):
    grad_ref[...] = rows_ref[...]
    total = parts_ref[:8, :]
    for z in range(1, 12):
        total = total + parts_ref[8 * z : 8 * z + 8, :]
    sum_ref[...] = total


def kernel_call(body, outs, in_specs, cost):
    return pl.pallas_call(
        body,
        out_shape=outs,
        in_specs=in_specs,
        out_specs=[VMEM] * len(outs),
        compiler_params=pltpu.CompilerParams(vmem_limit_bytes=16 * 2**20),
        cost_estimate=pl.CostEstimate(flops=cost, bytes_accessed=cost, transcendentals=0),
    )


def exchange(value, axes):
    return lax.all_to_all(value, axes, split_axis=0, concat_axis=0, tiled=True)


def turned(value, steps):
    pairs = [(source, (source + steps) % N_QUARTER) for source in range(N_QUARTER)]
    return lax.ppermute(value, QUARTER, pairs)


def shape(*dims, dtype=F32):
    return jax.ShapeDtypeStruct(dims, dtype)


def program(text, vision, vision_token, gain, cotangent):
    device = jnp.full((1,), lax.axis_index(AXES), jnp.int32)
    tokens = exchange(
        jnp.broadcast_to(vision_token[None, :], (N_QUARTER * N_FSDP, VIS)), QUARTER + FSDP
    )
    rows = turned(vision, 1)

    sent, order, taken = kernel_call(
        pack_kernel,
        [shape(SLOTS, HALF + LANES, dtype=BF16), shape(2 * VIS, SLOTS, dtype=BF16), shape(8, TOK)],
        [SMEM, VMEM, VMEM, VMEM],
        2 * 2**20,
    )(device, tokens, gain.reshape(8, LANES), cotangent)
    arrived = exchange(sent, FSDP)

    values = text.astype(F32)
    inv = lax.rsqrt(jnp.mean(values * values, axis=-1, keepdims=True) + 1e-06)
    kept = jnp.where(taken[0][:, None] > 0.0, 0.0, inv)
    text_terms = jnp.sum(cotangent.astype(F32) * values * kept, axis=0)

    values_v = rows.astype(F32)
    inv_v = lax.rsqrt(jnp.mean(values_v * values_v, axis=-1, keepdims=True) + 1e-06)
    unit = values_v * inv_v
    terms, upper = kernel_call(
        terms_kernel, [shape(2 * BLOCKS, LANES), shape(VIS, WIDTH, dtype=BF16)], [VMEM] * 4, 2**20
    )(order, arrived, unit, text_terms.reshape(BLOCKS, LANES))
    (grad,) = kernel_call(grads_kernel, [shape(VIS, WIDTH, dtype=BF16)], [VMEM] * 4, 2**20)(
        arrived, upper, unit, jnp.broadcast_to(inv_v, (VIS, LANES))
    )
    vision_grad = turned(grad, -1)

    pieces = exchange(terms, PLANE)
    part = jnp.sum(pieces.reshape(64, 2, LANES), axis=0)
    parts = exchange(jnp.broadcast_to(part[None], (48, 2, LANES)).reshape(96, LANES), ZX)
    vision_grad, gain_grad = kernel_call(
        finish_kernel, [shape(VIS, WIDTH, dtype=BF16), shape(8, LANES)], [VMEM] * 2, 2**19
    )(parts, vision_grad)
    return (vision_grad, gain_grad.reshape(WIDTH // N_FSDP))


def solution(mesh):
    fine = Mesh(mesh.devices.reshape(SIZES), AXES)
    return jax.shard_map(
        program,
        mesh=fine,
        in_specs=(P(AXES, None), P(AXES, None), P(AXES), P(FSDP), P(AXES, None)),
        out_specs=(P(AXES, None), P(FSDP)),
        check_vma=False,
    )
```

```python
import jax
import jax.numpy as jnp
from jax import lax
from jax.experimental import pallas as pl
from jax.experimental.pallas import tpu as pltpu
from jax.sharding import Mesh, PartitionSpec as P

AXES = ("ylo", "zhi", "zlo", "x", "yhi", "core")
QUARTER = ("ylo", "zhi")
ZX = ("zhi", "zlo", "x")
FSDP = ("yhi", "core")
PLANE = ("yhi", "core", "ylo", "x")
SIZES = (2, 2, 6, 4, 4, 2)
DEVICES = 768
N_QUARTER = 4
N_FSDP = 8
CAP = 4
TOK = 128
VIS = 16
WIDTH = 8192
HALF = WIDTH // 2
LANES = 128
SLOTS = N_FSDP * 2 * CAP
BLOCKS = WIDTH // LANES
F32 = jnp.float32
BF16 = jnp.bfloat16
VMEM = pl.BlockSpec(memory_space=pltpu.VMEM)
SMEM = pl.BlockSpec(memory_space=pltpu.SMEM)


def iota(shape, dim):
    return lax.broadcasted_iota(jnp.int32, shape, dim)


def dot(a, b):
    return jnp.dot(a, b, preferred_element_type=F32)


def pack_kernel(dev_ref, tok_ref, gain_ref, cot_ref, sent_ref, order_ref, taken_ref):
    dev = dev_ref[0]
    source = lax.rem(dev // (DEVICES // N_QUARTER) + N_QUARTER - 1, N_QUARTER) * N_FSDP
    tokens = tok_ref[pl.ds(pl.multiple_of(source, N_FSDP), N_FSDP), :]
    position = dev * TOK + iota((N_FSDP, TOK), 1)
    count = jnp.zeros((N_FSDP, TOK), jnp.int32)
    chosen = [jnp.zeros((N_FSDP, TOK), F32)] * CAP
    for i in range(VIS):
        token = jnp.broadcast_to(tokens[:, i : i + 1], (N_FSDP, TOK))
        hit = token == position
        for r in range(CAP):
            chosen[r] = jnp.where(hit & (count == r), 1.0, chosen[r])
        count = count + jnp.where((token >> 7) == dev, 1, 0)
    chosen = jnp.concatenate(chosen, axis=0)
    taken_ref[...] = jnp.broadcast_to(jnp.sum(chosen, axis=0, keepdims=True), taken_ref.shape)
    chosen = chosen.astype(BF16)
    row, col = iota((SLOTS, N_FSDP * CAP), 0), iota((SLOTS, N_FSDP * CAP), 1)
    halves = []
    for half in range(2):
        at = ((col & 7) == (row >> 3)) & ((col >> 3) + CAP * half == (row & 7))
        halves.append(dot(jnp.where(at, 1.0, 0.0).astype(BF16), chosen).astype(BF16))
    lhs = jnp.concatenate(halves, axis=1)
    step = 512
    for k in range(0, HALF, step):
        rhs = jnp.concatenate([cot_ref[:, k : k + step], cot_ref[:, HALF + k : HALF + k + step]], axis=0)
        sent_ref[:, k : k + step] = dot(lhs, rhs).astype(BF16)
    gain = gain_ref[...].astype(F32)
    sent_ref[:, HALF:] = jnp.concatenate([gain] * N_FSDP, axis=0).astype(BF16)
    own = jnp.broadcast_to(tok_ref[pl.ds(source + lax.rem(dev, N_FSDP), 1), :], (VIS, VIS))
    i, j = iota((VIS, VIS), 0), iota((VIS, VIS), 1)
    target = ((own >> 7) & (N_FSDP - 1)).astype(F32)
    mine = jnp.sum(jnp.where(i == j, target, 0.0), axis=1, keepdims=True)
    rank = jnp.sum(jnp.where((target == mine) & (j < i), 1.0, 0.0), axis=1, keepdims=True)
    slot = (mine * 8.0 + rank).astype(jnp.int32)
    at = iota((VIS, SLOTS), 1)
    order = [jnp.where(at == slot + CAP * half, 1.0, 0.0) for half in range(2)]
    order_ref[...] = jnp.concatenate(order, axis=0).astype(BF16)


def terms_kernel(order_ref, arrived_ref, unit_ref, text_ref, terms_ref, upper_ref):
    step = 8 * LANES
    for k in range(0, WIDTH, step):
        half, at = divmod(k, HALF)
        upper = dot(order_ref[half * VIS : (half + 1) * VIS, :], arrived_ref[:, at : at + step])
        upper_ref[:, k : k + step] = upper.astype(BF16)
        product = upper * unit_ref[:, k : k + step]
        total = jnp.sum(product, axis=0, keepdims=True)
        block = k // LANES
        rows = [total[:, b * LANES : (b + 1) * LANES] for b in range(8)]
        rows = text_ref[block : block + 8, :] + jnp.concatenate(rows, axis=0)
        terms_ref[2 * block : 2 * block + 8, :] = rows
        terms_ref[2 * block + 8 : 2 * block + 16, :] = rows


def grads_kernel(arrived_ref, upper_ref, unit_ref, inv_ref, grad_ref):
    total = jnp.zeros((VIS, LANES), F32)
    for b in range(BLOCKS):
        at = slice(b * LANES, (b + 1) * LANES)
        gain = arrived_ref[b : b + 1, HALF:].astype(F32)
        total = total + upper_ref[:, at].astype(F32) * gain * unit_ref[:, at]
    inner = jnp.sum(total, axis=1, keepdims=True) * (1.0 / WIDTH)
    inv = inv_ref[...]
    for b in range(BLOCKS):
        at = slice(b * LANES, (b + 1) * LANES)
        gain = arrived_ref[b : b + 1, HALF:].astype(F32)
        scaled = upper_ref[:, at].astype(F32) * gain
        grad_ref[:, at] = (inv * (scaled - unit_ref[:, at] * inner)).astype(BF16)


def repeat_kernel(pieces_ref, parts_ref):
    total = pieces_ref[:8, :]
    for k in range(8, 2 * BLOCKS, 8):
        total = total + pieces_ref[k : k + 8, :]
    total = total + pltpu.roll(total, 4, 0)
    total = total + pltpu.roll(total, 2, 0)
    for k in range(0, 96, 8):
        parts_ref[k : k + 8, :] = total


def finish_kernel(parts_ref, rows_ref, grad_ref, sum_ref, sem):
    copy = pltpu.make_async_copy(rows_ref, grad_ref, sem)
    copy.start()
    total = parts_ref[:8, :]
    for z in range(1, 12):
        total = total + parts_ref[8 * z : 8 * z + 8, :]
    sum_ref[...] = total
    copy.wait()


def kernel_call(body, outs, in_specs, cost, out_specs=None, scratch=()):
    return pl.pallas_call(
        body,
        out_shape=outs,
        in_specs=in_specs,
        out_specs=out_specs or [VMEM] * len(outs),
        scratch_shapes=scratch,
        compiler_params=pltpu.CompilerParams(vmem_limit_bytes=16 * 2**20),
        cost_estimate=pl.CostEstimate(flops=cost, bytes_accessed=cost, transcendentals=0),
    )


def exchange(value, axes):
    return lax.all_to_all(value, axes, split_axis=0, concat_axis=0, tiled=True)


def turned(value, steps):
    pairs = [(source, (source + steps) % N_QUARTER) for source in range(N_QUARTER)]
    return lax.ppermute(value, QUARTER, pairs)


def shape(*dims, dtype=F32):
    return jax.ShapeDtypeStruct(dims, dtype)


def program(text, vision, vision_token, gain, cotangent):
    device = jnp.full((1,), lax.axis_index(AXES), jnp.int32)
    tokens = exchange(
        jnp.broadcast_to(vision_token[None, :], (N_QUARTER * N_FSDP, VIS)), QUARTER + FSDP
    )
    rows = turned(vision, 1)

    sent, order, taken = kernel_call(
        pack_kernel,
        [shape(SLOTS, HALF + LANES, dtype=BF16), shape(2 * VIS, SLOTS, dtype=BF16), shape(8, TOK)],
        [SMEM, VMEM, VMEM, VMEM],
        2 * 2**20,
    )(device, tokens, gain.reshape(8, LANES), cotangent)
    arrived = exchange(sent, FSDP)

    values = text.astype(F32)
    inv = lax.rsqrt(jnp.mean(values * values, axis=-1, keepdims=True) + 1e-06)
    kept = jnp.where(taken[0][:, None] > 0.0, 0.0, inv)
    text_terms = jnp.sum(cotangent.astype(F32) * values * kept, axis=0)

    values_v = rows.astype(F32)
    inv_v = lax.rsqrt(jnp.mean(values_v * values_v, axis=-1, keepdims=True) + 1e-06)
    unit = values_v * inv_v
    terms, upper = kernel_call(
        terms_kernel, [shape(2 * BLOCKS, LANES), shape(VIS, WIDTH, dtype=BF16)], [VMEM] * 4, 2**20
    )(order, arrived, unit, text_terms.reshape(BLOCKS, LANES))
    (grad,) = kernel_call(grads_kernel, [shape(VIS, WIDTH, dtype=BF16)], [VMEM] * 4, 2**20)(
        arrived, upper, unit, jnp.broadcast_to(inv_v, (VIS, LANES))
    )
    vision_grad = turned(grad, -1)

    pieces = exchange(terms, PLANE)
    (part,) = kernel_call(repeat_kernel, [shape(96, LANES)], [VMEM], 2**16)(pieces)
    parts = exchange(part, ZX)
    vision_grad, gain_grad = kernel_call(
        finish_kernel, [shape(VIS, WIDTH, dtype=BF16), shape(8, LANES)], [VMEM] * 2, 2**19,
        [pl.BlockSpec(memory_space=pl.ANY), VMEM], [pltpu.SemaphoreType.DMA]
    )(parts, vision_grad)
    return (vision_grad, gain_grad.reshape(WIDTH // N_FSDP))


def solution(mesh):
    fine = Mesh(mesh.devices.reshape(SIZES), AXES)
    return jax.shard_map(
        program,
        mesh=fine,
        in_specs=(P(AXES, None), P(AXES, None), P(AXES), P(FSDP), P(AXES, None)),
        out_specs=(P(AXES, None), P(FSDP)),
        check_vma=False,
    )
```
